128 devices in a mesh: row: 16 (over y_hi, x, core), blk: 2 (over y_lo), grp: 4 (over z).
Axes of the slice: x: 4, y: 4 (y_hi: 2, y_lo: 2; y = y_hi * 2 + y_lo), z: 4, core: 2. Of those that a mesh axis runs over, the one named last changes fastest.
Arguments:
- column_slab: bfloat16 [16384, 8192], P('row', ('blk', 'grp')), may hold values from -36 to 36
Outputs:
- rotated_slab: bfloat16 [16384, 8192], P('row', ('blk', 'grp'))
The draws below stay inside these ranges and needn't reach their ends.
All inputs are finite; a program needn't handle non-finite values.
Results may differ from the reference program's by a relative error of at most 0.0049.
Values may be sent and summed in bfloat16 or wider, within the bound.
No kernel may reach another device: no remote copies, remote signals or barrier semaphores. Data moves between devices by JAX's collectives and lax.ppermute only.
A program may use at most 320 MiB of HBM per device.

```python
import jax
import jax.numpy as jnp
from jax import lax

N = 8192
B = 256
STEPS = 1
INNER = 2
M = 16384


def draw_column_slab(key, part):
    key_rows, key_cols, key_base = jax.random.split(key, 3)
    positions = jnp.arange(M, dtype=jnp.float32)
    row_scale = jnp.exp(jnp.log(3.0) * positions / M) * jnp.exp(jax.random.uniform(key_rows, (M,), jnp.float32, 0.0, jnp.log(4.0)))
    col_scale = jnp.exp(jax.random.uniform(key_cols, (N,), jnp.float32, jnp.log(0.3), jnp.log(3.0)))
    base = jnp.clip(jax.random.normal(key_base, (M, N), jnp.float32), -4.0, 4.0)
    return (base * row_scale[:, None] * col_scale[None, :] * 0.25).astype(jnp.bfloat16)


def setup_inputs(seed: int = 0) -> dict:
    keys = jax.random.split(jax.random.key(seed), 2)
    return {
        "column_slab": draw_column_slab(jax.random.fold_in(keys[1], 71), 0),
    }


def batched_dot(left_side, right_side):
    return jnp.einsum('pij,pjk->pik', left_side, right_side, precision=lax.Precision.HIGHEST)

def flipped(matrix):
    return jnp.swapaxes(matrix, 1, 2)

def cayley(current):
    half = current.shape[-1] // 2
    upper_block = current[:, :half, :half]
    lower_block = current[:, half:, half:]
    cross_block = current[:, :half, half:]
    diagonal_entries = jnp.diagonal(current, axis1=1, axis2=2)
    diag_mean = jnp.mean(diagonal_entries, axis=1) + 1e-06
    gradient = batched_dot(upper_block, cross_block) - batched_dot(cross_block, lower_block)
    coupling = -gradient / (diag_mean * diag_mean)[:, None, None]
    identity = jnp.broadcast_to(jnp.eye(half, dtype=jnp.float32), coupling.shape)
    outer_left = batched_dot(coupling, flipped(coupling))
    outer_right = batched_dot(flipped(coupling), coupling)
    factor_left = jnp.linalg.cholesky(identity + outer_left)
    factor_right = jnp.linalg.cholesky(identity + outer_right)
    left_part = jax.scipy.linalg.cho_solve((factor_left, True), jnp.concatenate([identity - outer_left, -2.0 * coupling], axis=2))
    right_part = jax.scipy.linalg.cho_solve((factor_right, True), jnp.concatenate([2.0 * flipped(coupling), identity - outer_right], axis=2))
    return flipped(jnp.concatenate([left_part, right_part], axis=1))

def rotation(gram_blocks):
    current = gram_blocks
    accumulated = None
    for sweep_index in range(INNER):
        rotor = cayley(current)
        accumulated = rotor if sweep_index == 0 else batched_dot(accumulated, rotor)
        if sweep_index + 1 < INNER:
            current = batched_dot(flipped(rotor), batched_dot(current, rotor))
    return accumulated.astype(jnp.bfloat16)

def gram_of(pair_item):
    return jnp.dot(pair_item.T.astype(jnp.float32), pair_item.astype(jnp.float32), preferred_element_type=jnp.float32)

def rotate_one(pair_entry):
    return jnp.dot(pair_entry[0].astype(jnp.float32), pair_entry[1].astype(jnp.float32), preferred_element_type=jnp.float32).astype(jnp.bfloat16)

def reference(column_slab):
    pair_total = N // (2 * B)
    pair_cols = column_slab.reshape(M, pair_total, 2 * B).transpose(1, 0, 2)
    for section_index in range(STEPS):
        gram_blocks = lax.map(gram_of, pair_cols)
        rotors = rotation(gram_blocks)
        pair_cols = lax.map(rotate_one, (pair_cols, rotors))
        upper_half = pair_cols[:, :, :B]
        lower_half = pair_cols[:, :, B:]
        new_upper = jnp.concatenate([upper_half[:1], lower_half[:1], upper_half[1:-1]], axis=0)
        new_lower = jnp.concatenate([lower_half[1:], upper_half[-1:]], axis=0)
        pair_cols = jnp.concatenate([new_upper, new_lower], axis=2)
    return pair_cols.transpose(1, 0, 2).reshape(M, N)
```

```python
import jax
import jax.numpy as jnp
from jax import lax
from jax.experimental import pallas as pl
from jax.experimental.pallas import tpu as pltpu
from jax.sharding import Mesh, PartitionSpec as P

B = 256
PAIR = 2 * B
INNER = 2
T = 128
BLOCKS = ((0, 0), (0, 1), (1, 1), (0, 2), (0, 3), (1, 2), (1, 3), (2, 2), (2, 3), (3, 3))
PACKED = len(BLOCKS) * T
XS = 4
CHUNK = PACKED // XS
PIECE = 64
BF = jnp.bfloat16
F32 = jnp.float32
VMEM_LIMIT = 48 << 20


def params():
    return pltpu.CompilerParams(vmem_limit_bytes=VMEM_LIMIT)


def dot(a, b):
    return lax.dot_general(a, b, (((1,), (0,)), ((), ())), preferred_element_type=F32)


def dot_tn(a, b):
    return lax.dot_general(a, b, (((0,), (0,)), ((), ())), preferred_element_type=F32)


def split(x):
    hi = x.astype(BF)
    return hi, (x - hi.astype(F32)).astype(BF)


def mul(a, b):
    return dot(a[0], b[0]) + (dot(a[0], b[1]) + dot(a[1], b[0]))


def gram_kernel(idx_ref, a_ref, out_ref, acc_ref):
    step = pl.program_id(0)
    upper, lower = a_ref[:, :B], a_ref[:, B:]
    pp, pq, qq = dot_tn(upper, upper), dot_tn(upper, lower), dot_tn(lower, lower)

    @pl.when(step == 0)
    def _():
        acc_ref[0] = pp
        acc_ref[1] = pq
        acc_ref[2] = qq

    @pl.when(step > 0)
    def _():
        acc_ref[0] += pp
        acc_ref[1] += pq
        acc_ref[2] += qq

    @pl.when(step == pl.num_programs(0) - 1)
    def _():
        xi = idx_ref[1]
        for q in range(PACKED // PIECE):
            row, col = BLOCKS[q * PIECE // T]
            part = q * PIECE % T
            which = row // 2 + col // 2
            r0, c0 = row % 2 * T + part, col % 2 * T
            chunk, offset = divmod(q * PIECE, CHUNK)
            place = lax.rem(chunk - xi + XS, XS) * CHUNK + offset
            out_ref[pl.ds(pl.multiple_of(place, PIECE), PIECE), :] = acc_ref[
                which, r0 : r0 + PIECE, c0 : c0 + T
            ]


def gram(slab, pair, xi):
    rows = slab.shape[0]
    tile = 256
    return pl.pallas_call(
        gram_kernel,
        out_shape=jax.ShapeDtypeStruct((PACKED, T), F32),
        grid_spec=pltpu.PrefetchScalarGridSpec(
            num_scalar_prefetch=1,
            grid=(rows // tile,),
            in_specs=[pl.BlockSpec((tile, PAIR), lambda i, idx: (i, idx[0]))],
            out_specs=pl.BlockSpec((PACKED, T), lambda i, idx: (0, 0)),
            scratch_shapes=[pltpu.VMEM((3, B, B), F32)],
        ),
        compiler_params=params(),
        name="gram",
    )(jnp.stack([pair, xi]).astype(jnp.int32), slab)


def inverse(gramian, eye):
    top = jnp.sqrt(jnp.sum(gramian * gramian))
    scale = 2.0 / (2.0 + top)
    gap = scale
    rest = eye - scale * (eye + gramian)

    def more(state):
        count, gap, _, _ = state
        return (gap < 1.0 - 1e-6) & (count < 60)

    def step(state):
        count, gap, rest, approx = state
        rate = 1.0 - gap
        c = 2.0 / (2.0 - rate * rate)
        parts = split(rest)
        square = mul(parts, parts)
        approx = c * (approx + mul(split(approx), parts))
        rest = c * square + (1.0 - c) * eye
        gap = 2.0 * gap * (2.0 - gap) / (1.0 + gap * (2.0 - gap))
        return count + 1, gap, rest, approx

    state = (jnp.int32(0), gap, rest, scale * eye)
    return lax.while_loop(more, step, state)[3]


def rotation_kernel(idx_ref, g0_ref, g1_ref, g2_ref, g3_ref, out_ref, pack_ref, h_ref, e_ref):
    xi = idx_ref[0]
    for i, ref in enumerate((g0_ref, g1_ref, g2_ref, g3_ref)):
        place = lax.rem(xi - i + XS, XS) * CHUNK
        pack_ref[pl.ds(pl.multiple_of(place, PIECE), CHUNK), :] = ref[...]
    for b, (row, col) in enumerate(BLOCKS):
        block = pack_ref[b * T : (b + 1) * T, :]
        h_ref[row * T : (row + 1) * T, col * T : (col + 1) * T] = block
        if row != col:
            h_ref[col * T : (col + 1) * T, row * T : (row + 1) * T] = block.T
    rows = lax.broadcasted_iota(jnp.int32, (B, B), 0)
    cols = lax.broadcasted_iota(jnp.int32, (B, B), 1)
    eye = jnp.where(rows == cols, 1.0, 0.0).astype(F32)

    for sweep in range(INNER):
        trace = jnp.sum((h_ref[:B, :B] + h_ref[B:, B:]) * eye)
        mean = trace / PAIR + 1e-6
        factor = -1.0 / (mean * mean)
        pp, pq = split(h_ref[:B, :B]), split(h_ref[:B, B:])
        qp, qq = split(h_ref[B:, :B]), split(h_ref[B:, B:])
        x = split((mul(pp, pq) - mul(pq, qq)) * factor)
        xt = split((mul(qp, pp) - mul(qq, qp)) * factor)
        pi = inverse(mul(x, xt), eye)
        pis = split(pi)
        w = mul(pis, x)
        wt = mul(xt, pis)
        t = mul(split(wt), x)
        e = jnp.concatenate(
            [
                jnp.concatenate([2.0 * (pi - eye), 2.0 * w], axis=1),
                jnp.concatenate([-2.0 * wt, -2.0 * t], axis=1),
            ],
            axis=0,
        )
        if sweep == 0:
            e_ref[...] = e
            et = jnp.concatenate(
                [
                    jnp.concatenate([2.0 * (pi - eye), -2.0 * w], axis=1),
                    jnp.concatenate([2.0 * wt, -2.0 * t], axis=1),
                ],
                axis=0,
            )
            h = h_ref[...]
            m = h + mul(split(h), split(e))
            h_ref[...] = m + mul(split(et), split(m))
        else:
            first = e_ref[...]
            r = lax.broadcasted_iota(jnp.int32, (PAIR, PAIR), 0)
            c = lax.broadcasted_iota(jnp.int32, (PAIR, PAIR), 1)
            whole = jnp.where(r == c, 1.0, 0.0).astype(F32)
            v = whole + (first + e) + mul(split(first), split(e))
            out_ref[...] = v.astype(BF)


def rotation(chunks, xi):
    spec = pl.BlockSpec((CHUNK, T), lambda i, idx: (0, 0))
    return pl.pallas_call(
        rotation_kernel,
        out_shape=jax.ShapeDtypeStruct((PAIR, PAIR), BF),
        grid_spec=pltpu.PrefetchScalarGridSpec(
            num_scalar_prefetch=1,
            grid=(1,),
            in_specs=[spec] * XS,
            out_specs=pl.BlockSpec((PAIR, PAIR), lambda i, idx: (0, 0)),
            scratch_shapes=[
                pltpu.VMEM((PACKED, T), F32),
                pltpu.VMEM((PAIR, PAIR), F32),
                pltpu.VMEM((PAIR, PAIR), F32),
            ],
        ),
        compiler_params=params(),
        name="rotation",
    )(xi.reshape(1).astype(jnp.int32), *chunks)


def apply_kernel(idx_ref, a_ref, own_ref, other_ref, out_ref, up_ref, down_ref, rot_ref):
    core, position = idx_ref[0], idx_ref[1]

    @pl.when(pl.program_id(0) == 0)
    def _():
        rot_ref[core] = own_ref[...]
        rot_ref[1 - core] = other_ref[...]

    first = dot(a_ref[:, :PAIR], rot_ref[0]).astype(BF)
    second = dot(a_ref[:, PAIR:], rot_ref[1]).astype(BF)
    out_ref[:, :B] = first[:, :B]
    out_ref[:, B:PAIR] = second[:, B:]
    out_ref[:, PAIR + B :] = second[:, :B]

    @pl.when(position == 0)
    def _():
        out_ref[:, PAIR : PAIR + B] = first[:, B:]

    @pl.when(position > 0)
    def _():
        out_ref[:, PAIR : PAIR + B] = first[:, :B]

    up_ref[...] = second[:, :B]
    down_ref[...] = first[:, B:]


def apply(slab, own, other, core, position):
    rows, cols = slab.shape
    tile = 256
    fixed = pl.BlockSpec((PAIR, PAIR), lambda i, idx: (0, 0))
    half = pl.BlockSpec((tile, B), lambda i, idx: (i, 0))
    full = pl.BlockSpec((tile, cols), lambda i, idx: (i, 0))
    return pl.pallas_call(
        apply_kernel,
        out_shape=(
            jax.ShapeDtypeStruct((rows, cols), BF),
            jax.ShapeDtypeStruct((rows, B), BF),
            jax.ShapeDtypeStruct((rows, B), BF),
        ),
        grid_spec=pltpu.PrefetchScalarGridSpec(
            num_scalar_prefetch=1,
            grid=(rows // tile,),
            in_specs=[full, fixed, fixed],
            out_specs=(full, half, half),
            scratch_shapes=[pltpu.VMEM((2, PAIR, PAIR), BF)],
        ),
        compiler_params=params(),
        name="apply",
    )(jnp.stack([core, position]).astype(jnp.int32), slab, own, other)


def finish_kernel(last, idx_ref, before_ref, after_ref, part_ref, out_ref, sems):
    del part_ref
    position = idx_ref[0]

    def low():
        return pltpu.make_async_copy(before_ref, out_ref.at[:, pl.ds(0, B)], sems.at[0])

    def high():
        return pltpu.make_async_copy(after_ref, out_ref.at[:, pl.ds(PAIR + B, B)], sems.at[1])

    @pl.when(position > 0)
    def _():
        low().start()

    @pl.when(position < last)
    def _():
        high().start()

    @pl.when(position > 0)
    def _():
        low().wait()

    @pl.when(position < last)
    def _():
        high().wait()


def finish(part, before, after, position, last):
    anywhere = pl.BlockSpec(memory_space=pl.ANY)
    return pl.pallas_call(
        lambda *refs: finish_kernel(last, *refs),
        out_shape=jax.ShapeDtypeStruct(part.shape, part.dtype),
        grid_spec=pltpu.PrefetchScalarGridSpec(
            num_scalar_prefetch=1,
            grid=(1,),
            in_specs=[anywhere] * 3,
            out_specs=anywhere,
            scratch_shapes=[pltpu.SemaphoreType.DMA((2,))],
        ),
        input_output_aliases={3: 0},
        compiler_params=params(),
        name="finish",
    )(position.reshape(1).astype(jnp.int32), before, after, part)


def shifted(array, axis, by):
    size = lax.axis_size(axis)
    return lax.ppermute(array, axis, [(i, (i + by) % size) for i in range(size)])


def body(slab):
    core, xi = lax.axis_index("core"), lax.axis_index("x")
    chain = ("blk", "grp")
    size, position = lax.axis_size(chain), lax.axis_index(chain)

    theirs = gram(slab, 1 - core, xi)
    received = shifted(theirs, "core", 1)
    packed = gram(slab, core, xi) + received

    total = packed[:CHUNK]
    parts = [
        shifted(packed[i * CHUNK : (i + 1) * CHUNK], "x", i) for i in range(1, XS)
    ]
    total = total + parts[0] + parts[1] + parts[2]
    total = total + shifted(total, "yh", 1)
    chunks = [total] + [shifted(total, "x", i) for i in range(1, XS)]

    own = rotation(chunks, xi)
    other = shifted(own, "core", 1)
    part, up, down = apply(slab, own, other, core, position)
    before = lax.ppermute(up, chain, [(i, i + 1) for i in range(size - 1)])
    after = lax.ppermute(down, chain, [(i, i - 1) for i in range(1, size)])
    return finish(part, before, after, position, size - 1)


def solution(mesh):
    rows, blk, grp = (mesh.shape[name] for name in ("row", "blk", "grp"))
    fine = Mesh(
        mesh.devices.reshape(rows // (2 * XS), XS, 2, blk, grp),
        ("yh", "x", "core", "blk", "grp"),
    )
    spec = P(("yh", "x", "core"), ("blk", "grp"))
    return jax.shard_map(
        body, mesh=fine, in_specs=(spec,), out_specs=spec, check_vma=False
    )
```

```python
import jax
import jax.numpy as jnp
from jax import lax
from jax.experimental import pallas as pl
from jax.experimental.pallas import tpu as pltpu
from jax.sharding import Mesh, PartitionSpec as P


B = 256
PAIR = 2 * B
INNER = 2
T = 128
BLOCKS = ((0, 0), (0, 1), (1, 1), (0, 2), (0, 3), (1, 2), (1, 3), (2, 2), (2, 3), (3, 3))
PACKED = len(BLOCKS) * T
XS = 4
CHUNK = PACKED // XS
PIECE = 64
TAIL = 16
SPAN = CHUNK + TAIL
BF = jnp.bfloat16
F32 = jnp.float32
VMEM_LIMIT = 48 << 20
ROW_TILE = 256
TOP_EXPONENT = 14.0


def params():
    return pltpu.CompilerParams(vmem_limit_bytes=VMEM_LIMIT)


def dot(a, b):
    return lax.dot_general(a, b, (((1,), (0,)), ((), ())), preferred_element_type=F32)


def dot_tn(a, b):
    return lax.dot_general(a, b, (((0,), (0,)), ((), ())), preferred_element_type=F32)


def split(x):
    hi = x.astype(BF)
    return hi, (x - hi.astype(F32)).astype(BF)


def mul(a, b):
    return dot(a[0], b[0]) + (dot(a[0], b[1]) + dot(a[1], b[0]))


def gram_kernel(idx_ref, a_ref, out_ref, acc_ref):
    step = pl.program_id(0)
    upper, lower = a_ref[:, :B], a_ref[:, B:]
    pp, pq, qq = dot_tn(upper, upper), dot_tn(upper, lower), dot_tn(lower, lower)

    @pl.when(step == 0)
    def _():
        acc_ref[0] = pp
        acc_ref[1] = pq
        acc_ref[2] = qq

    @pl.when(step > 0)
    def _():
        acc_ref[0] += pp
        acc_ref[1] += pq
        acc_ref[2] += qq

    @pl.when(step == pl.num_programs(0) - 1)
    def _():
        xi = idx_ref[1]
        top = jnp.zeros((TAIL, T), F32)
        for q in range(PACKED // PIECE):
            row, col = BLOCKS[q * PIECE // T]
            part = q * PIECE % T
            which = row // 2 + col // 2
            r0, c0 = row % 2 * T + part, col % 2 * T
            chunk, offset = divmod(q * PIECE, CHUNK)
            place = lax.rem(chunk - xi + XS, XS) * SPAN + offset
            piece = acc_ref[which, r0 : r0 + PIECE, c0 : c0 + T]
            out_ref[pl.ds(pl.multiple_of(place, TAIL), PIECE), :] = piece
            for r in range(0, PIECE, TAIL):
                top = jnp.maximum(top, jnp.abs(piece[r : r + TAIL]))
        top = jnp.broadcast_to(jnp.max(top, axis=0, keepdims=True), (TAIL, T))
        for i in range(XS):
            out_ref[i * SPAN + CHUNK : (i + 1) * SPAN, :] = top


def gram(slab, pair, xi):
    rows = slab.shape[0]
    tile = 256
    return pl.pallas_call(
        gram_kernel,
        out_shape=jax.ShapeDtypeStruct((XS * SPAN, T), F32),
        grid_spec=pltpu.PrefetchScalarGridSpec(
            num_scalar_prefetch=1,
            grid=(rows // tile,),
            in_specs=[pl.BlockSpec((tile, PAIR), lambda i, idx: (i, idx[0]))],
            out_specs=pl.BlockSpec((XS * SPAN, T), lambda i, idx: (0, 0)),
            scratch_shapes=[pltpu.VMEM((3, B, B), F32)],
        ),
        compiler_params=params(),
        name="gram",
    )(jnp.stack([pair, xi]).astype(jnp.int32), slab)


def inverse(gramian, eye):
    top = jnp.sqrt(jnp.sum(gramian * gramian))
    scale = 2.0 / (2.0 + top)
    gap = scale
    rest = eye - scale * (eye + gramian)

    def more(state):
        count, gap, _, _ = state
        return (gap < 1.0 - 1e-6) & (count < 60)

    def step(state):
        count, gap, rest, approx = state
        rate = 1.0 - gap
        c = 2.0 / (2.0 - rate * rate)
        parts = split(rest)
        square = mul(parts, parts)
        approx = c * (approx + mul(split(approx), parts))
        rest = c * square + (1.0 - c) * eye
        gap = 2.0 * gap * (2.0 - gap) / (1.0 + gap * (2.0 - gap))
        return count + 1, gap, rest, approx

    state = (jnp.int32(0), gap, rest, scale * eye)
    return lax.while_loop(more, step, state)[3]


def rotation_kernel(idx_ref, g0_ref, g1_ref, g2_ref, g3_ref, out_ref, pack_ref, h_ref, e_ref):
    xi = idx_ref[0]
    for i, ref in enumerate((g0_ref, g1_ref, g2_ref, g3_ref)):
        place = lax.rem(xi - i + XS, XS) * CHUNK
        pack_ref[pl.ds(pl.multiple_of(place, PIECE), CHUNK), :] = ref[:CHUNK, :]
    for b, (row, col) in enumerate(BLOCKS):
        block = pack_ref[b * T : (b + 1) * T, :]
        h_ref[row * T : (row + 1) * T, col * T : (col + 1) * T] = block
        if row != col:
            h_ref[col * T : (col + 1) * T, row * T : (row + 1) * T] = block.T
    rows = lax.broadcasted_iota(jnp.int32, (B, B), 0)
    cols = lax.broadcasted_iota(jnp.int32, (B, B), 1)
    eye = jnp.where(rows == cols, 1.0, 0.0).astype(F32)

    for sweep in range(INNER):
        trace = jnp.sum((h_ref[:B, :B] + h_ref[B:, B:]) * eye)
        mean = trace / PAIR + 1e-6
        factor = -1.0 / (mean * mean)
        pp, pq = split(h_ref[:B, :B]), split(h_ref[:B, B:])
        qp, qq = split(h_ref[B:, :B]), split(h_ref[B:, B:])
        x = split((mul(pp, pq) - mul(pq, qq)) * factor)
        xt = split((mul(qp, pp) - mul(qq, qp)) * factor)
        pi = inverse(mul(x, xt), eye)
        pis = split(pi)
        w = mul(pis, x)
        wt = mul(xt, pis)
        t = mul(split(wt), x)
        e = jnp.concatenate(
            [
                jnp.concatenate([2.0 * (pi - eye), 2.0 * w], axis=1),
                jnp.concatenate([-2.0 * wt, -2.0 * t], axis=1),
            ],
            axis=0,
        )
        if sweep == 0:
            e_ref[...] = e
            et = jnp.concatenate(
                [
                    jnp.concatenate([2.0 * (pi - eye), -2.0 * w], axis=1),
                    jnp.concatenate([2.0 * wt, -2.0 * t], axis=1),
                ],
                axis=0,
            )
            h = h_ref[...]
            m = h + mul(split(h), split(e))
            h_ref[...] = m + mul(split(et), split(m))
        else:
            first = e_ref[...]
            r = lax.broadcasted_iota(jnp.int32, (PAIR, PAIR), 0)
            c = lax.broadcasted_iota(jnp.int32, (PAIR, PAIR), 1)
            whole = jnp.where(r == c, 1.0, 0.0).astype(F32)
            v = whole + (first + e) + mul(split(first), split(e))
            out_ref[...] = v.astype(BF)


def rotation(chunks, xi):
    spec = pl.BlockSpec((SPAN, T), lambda i, idx: (0, 0))
    return pl.pallas_call(
        rotation_kernel,
        out_shape=jax.ShapeDtypeStruct((PAIR, PAIR), BF),
        grid_spec=pltpu.PrefetchScalarGridSpec(
            num_scalar_prefetch=1,
            grid=(1,),
            in_specs=[spec] * XS,
            out_specs=pl.BlockSpec((PAIR, PAIR), lambda i, idx: (0, 0)),
            scratch_shapes=[
                pltpu.VMEM((PACKED, T), F32),
                pltpu.VMEM((PAIR, PAIR), F32),
                pltpu.VMEM((PAIR, PAIR), F32),
            ],
        ),
        compiler_params=params(),
        name="rotation",
    )(xi.reshape(1).astype(jnp.int32), *chunks)


def whole(count):
    return [pl.BlockSpec(memory_space=pltpu.VMEM)] * count


def numbers(*values):
    return jnp.stack(values).astype(jnp.int32)


SCALARS = pl.BlockSpec(memory_space=pltpu.SMEM)
ANYWHERE = pl.BlockSpec(memory_space=pl.ANY)


def row_tiles(rows):
    return [pl.ds(i * ROW_TILE, ROW_TILE) for i in range(rows // ROW_TILE)]


def edge_kernel(idx_ref, a_ref, rot_ref, out_ref):
    columns = pl.ds(pl.multiple_of(idx_ref[0] * PAIR, PAIR), PAIR)
    rot = rot_ref[:, pl.ds(pl.multiple_of(idx_ref[1] * B, B), B)]
    for tile in row_tiles(a_ref.shape[0]):
        out_ref[tile, :] = dot(a_ref[tile, columns], rot).astype(BF)


def edge(slab, rot, pair, half):
    return pl.pallas_call(
        edge_kernel,
        out_shape=jax.ShapeDtypeStruct((slab.shape[0], B), BF),
        in_specs=[SCALARS] + whole(2),
        out_specs=whole(1)[0],
        compiler_params=params(),
        name="edge",
    )(numbers(pair, half), slab, rot)


def inner_kernel(last, idx_ref, a_ref, own_ref, other_ref, first_ref, out_ref, rot_ref, stage_ref, sems):
    core, position = idx_ref[0], idx_ref[1]
    tiles = row_tiles(a_ref.shape[0])

    def arrived(side):
        return pltpu.make_async_copy(
            first_ref, out_ref.at[:, pl.ds(side * (PAIR + B), B)], sems.at[len(tiles)]
        )

    def ended(i, side):
        columns = pl.ds(side * (PAIR + B), B)
        return pltpu.make_async_copy(
            stage_ref.at[tiles[i], columns],
            out_ref.at[tiles[i], columns],
            sems.at[len(tiles) + 1 + i],
        )

    goes = ((core == 1) & (position > 0), (core == 0) & (position < last))
    for side in range(2):

        @pl.when(goes[side])
        def _():
            arrived(side).start()

    rot_ref[core] = own_ref[...]
    rot_ref[1 - core] = other_ref[...]
    kept = rot_ref[1, :, B:]
    passed = rot_ref[0, :, pl.ds(pl.multiple_of(jnp.where(position == 0, B, 0), B), B)]
    middle = pl.ds(B, PAIR)
    copies = []
    for i, tile in enumerate(tiles):
        stage_ref[tile, B:PAIR] = dot(a_ref[tile, PAIR:], kept).astype(BF)
        stage_ref[tile, PAIR : PAIR + B] = dot(a_ref[tile, :PAIR], passed).astype(BF)
        copies.append(
            pltpu.make_async_copy(
                stage_ref.at[tile, middle], out_ref.at[tile, middle], sems.at[i]
            )
        )
        copies[-1].start()
    for side, place in ((0, 0), (1, last)):

        @pl.when(position == place)
        def _():
            rot = rot_ref[side, :, :B]
            for i, tile in enumerate(tiles):
                pair = a_ref[tile, side * PAIR : (side + 1) * PAIR]
                columns = slice(side * (PAIR + B), side * (PAIR + B) + B)
                stage_ref[tile, columns] = dot(pair, rot).astype(BF)
                ended(i, side).start()
            for i in range(len(tiles)):
                ended(i, side).wait()

    for copy in copies:
        copy.wait()
    for side in range(2):

        @pl.when(goes[side])
        def _():
            arrived(side).wait()


def inner(slab, own, other, first, core, position, last):
    count = slab.shape[0] // ROW_TILE
    return pl.pallas_call(
        lambda *refs: inner_kernel(last, *refs),
        out_shape=jax.ShapeDtypeStruct(slab.shape, BF),
        in_specs=[SCALARS] + whole(4),
        out_specs=ANYWHERE,
        scratch_shapes=[
            pltpu.VMEM((2, PAIR, PAIR), BF),
            pltpu.VMEM(slab.shape, BF),
            pltpu.SemaphoreType.DMA((2 * count + 1,)),
        ],
        compiler_params=params(),
        name="inner",
    )(numbers(core, position), slab, own, other, first)


def place_kernel(last, idx_ref, block_ref, part_ref, out_ref, sem):
    del part_ref
    core, position = idx_ref[0], idx_ref[1]
    goes = ((core == 0) & (position > 0), (core == 1) & (position < last))
    for side in range(2):

        @pl.when(goes[side])
        def _():
            copy = pltpu.make_async_copy(
                block_ref, out_ref.at[:, pl.ds(side * (PAIR + B), B)], sem.at[0]
            )
            copy.start()
            copy.wait()


def place(part, block, core, position, last):
    return pl.pallas_call(
        lambda *refs: place_kernel(last, *refs),
        out_shape=jax.ShapeDtypeStruct(part.shape, part.dtype),
        in_specs=[SCALARS] + whole(1) + [ANYWHERE],
        out_specs=ANYWHERE,
        scratch_shapes=[pltpu.SemaphoreType.DMA((1,))],
        input_output_aliases={2: 0},
        compiler_params=params(),
        name="place",
    )(numbers(core, position), block, part)


def shifted(array, axis, by):
    size = lax.axis_size(axis)
    return lax.ppermute(array, axis, [(i, (i + by) % size) for i in range(size)])


def along_chain(array, ups):
    size = lax.axis_size(("blk", "grp"))
    moves = []
    for core in range(2):
        for i in range(size - 1):
            pair = (core * size + i, core * size + i + 1)
            moves.append(pair if core in ups else pair[::-1])
    return lax.ppermute(array, ("core", "blk", "grp"), moves)


def encode(chunk):
    exponent = jnp.floor(jnp.log2(jnp.maximum(chunk[CHUNK : CHUNK + 1], 1e-30))) + 1.0
    rows = lax.broadcasted_iota(jnp.int32, chunk.shape, 0)
    scaled = chunk * jnp.exp2(TOP_EXPONENT - exponent)
    return jnp.where(rows < CHUNK, scaled, exponent).astype(jnp.float16)


def decode(message):
    message = message.astype(F32)
    exponent = message[CHUNK : CHUNK + 1]
    rows = lax.broadcasted_iota(jnp.int32, message.shape, 0)
    value = message * jnp.exp2(exponent - TOP_EXPONENT)
    return jnp.where(rows < CHUNK, value, jnp.exp2(exponent))


def body(slab):
    core, xi = lax.axis_index("core"), lax.axis_index("x")
    chain = ("blk", "grp")
    last, position = lax.axis_size(chain) - 1, lax.axis_index(chain)

    theirs = gram(slab, 1 - core, xi)
    received = shifted(theirs, "core", 1)
    packed = gram(slab, core, xi) + received

    total, *rest = (packed[i * SPAN : (i + 1) * SPAN] for i in range(XS))
    parts = [shifted(encode(part), "x", i) for i, part in enumerate(rest, 1)]
    for part in parts:
        total = total + decode(part)
    total = total + decode(shifted(encode(total), "yh", 1))
    coded = encode(total)
    chunks = [total] + [decode(shifted(coded, "x", i)) for i in range(1, XS)]

    own = rotation(chunks, xi)
    first = edge(slab, own, core, 1 - core)
    first = along_chain(first, (1,))
    other = shifted(own, "core", 1)
    second = edge(slab, other, 1 - core, core)
    second = along_chain(second, (0,))
    out = inner(slab, own, other, first, core, position, last)
    return place(out, second, core, position, last)


def solution(mesh):
    rows, blk, grp = (mesh.shape[name] for name in ("row", "blk", "grp"))
    fine = Mesh(
        mesh.devices.reshape(rows // (2 * XS), XS, 2, blk, grp),
        ("yh", "x", "core", "blk", "grp"),
    )
    spec = P(("yh", "x", "core"), ("blk", "grp"))
    return jax.shard_map(
        body, mesh=fine, in_specs=(spec,), out_specs=spec, check_vma=False
    )
```

```python
import jax
import jax.numpy as jnp
from jax import lax
from jax.experimental import pallas as pl
from jax.experimental.pallas import tpu as pltpu
from jax.sharding import Mesh, PartitionSpec as P


B = 256
PAIR = 2 * B
INNER = 2
T = 128
BLOCKS = ((0, 0), (0, 1), (1, 1), (0, 2), (0, 3), (1, 2), (1, 3), (2, 2), (2, 3), (3, 3))
PACKED = len(BLOCKS) * T
XS = 4
CHUNK = PACKED // XS
PIECE = 64
TAIL = 16
SPAN = CHUNK + TAIL
BF = jnp.bfloat16
F32 = jnp.float32
ROW_TILE = 256
TOP_EXPONENT = 14.0
ENOUGH = 2e-3


def params(mib=8):
    return pltpu.CompilerParams(vmem_limit_bytes=mib << 20)


def dot(a, b):
    return lax.dot_general(a, b, (((1,), (0,)), ((), ())), preferred_element_type=F32)


def dot_tn(a, b):
    return lax.dot_general(a, b, (((0,), (0,)), ((), ())), preferred_element_type=F32)


def split(x):
    hi = x.astype(BF)
    return hi, (x - hi.astype(F32)).astype(BF)


def mul(a, b):
    left = jnp.concatenate([a[0], a[0], a[1]], axis=1)
    return dot(left, jnp.concatenate([b[0], b[1], b[0]], axis=0))


def whole(count):
    return [pl.BlockSpec(memory_space=pltpu.VMEM)] * count


def numbers(*values):
    return jnp.stack(values).astype(jnp.int32)


SCALARS = pl.BlockSpec(memory_space=pltpu.SMEM)
ANYWHERE = pl.BlockSpec(memory_space=pl.ANY)


def row_tiles(rows):
    return [pl.ds(i * ROW_TILE, ROW_TILE) for i in range(rows // ROW_TILE)]


def pack(acc, xi, out_ref):
    top = jnp.zeros((TAIL, T), F32)
    for q in range(PACKED // PIECE):
        row, col = BLOCKS[q * PIECE // T]
        part = q * PIECE % T
        which = row // 2 + col // 2
        r0, c0 = row % 2 * T + part, col % 2 * T
        chunk, offset = divmod(q * PIECE, CHUNK)
        place = lax.rem(chunk - xi + XS, XS) * SPAN + offset
        piece = acc[which][r0 : r0 + PIECE, c0 : c0 + T]
        out_ref[pl.ds(pl.multiple_of(place, TAIL), PIECE), :] = piece
        for r in range(0, PIECE, TAIL):
            top = jnp.maximum(top, jnp.abs(piece[r : r + TAIL]))
    top = jnp.broadcast_to(jnp.max(top, axis=0, keepdims=True), (TAIL, T))
    for i in range(XS):
        out_ref[i * SPAN + CHUNK : (i + 1) * SPAN, :] = top


def products(rows):
    upper, lower = rows[:, :B], rows[:, B:]
    return dot_tn(upper, upper), dot_tn(upper, lower), dot_tn(lower, lower)


def first_gram_kernel(idx_ref, a_ref, out_ref, slab_ref, sems):
    pair, xi = idx_ref[0], idx_ref[1]
    tiles = row_tiles(a_ref.shape[0])

    def fetch(which, i):
        columns = pl.ds(pl.multiple_of(which * PAIR, PAIR), PAIR)
        return pltpu.make_async_copy(
            a_ref.at[tiles[i], columns], slab_ref.at[tiles[i], columns], sems.at[i]
        )

    def fetch_other(i):
        columns = pl.ds(pl.multiple_of((1 - pair) * PAIR, PAIR), PAIR)
        return pltpu.make_async_copy(
            a_ref.at[tiles[i], columns],
            slab_ref.at[tiles[i], columns],
            sems.at[len(tiles) + i],
        )

    for i in range(len(tiles)):
        fetch(pair, i).start()
    for i in range(len(tiles)):
        fetch_other(i).start()
    columns = pl.ds(pl.multiple_of(pair * PAIR, PAIR), PAIR)
    total = None
    for i, tile in enumerate(tiles):
        fetch(pair, i).wait()
        new = products(slab_ref[tile, columns])
        total = new if total is None else [x + y for x, y in zip(total, new)]
    pack(total, xi, out_ref)
    for i in range(len(tiles)):
        fetch_other(i).wait()


def first_gram(slab, pair, xi):
    count = slab.shape[0] // ROW_TILE
    return pl.pallas_call(
        first_gram_kernel,
        out_shape=(
            pltpu.VMEM((XS * SPAN, T), F32),
            pltpu.VMEM(slab.shape, slab.dtype),
        ),
        in_specs=[SCALARS, pl.BlockSpec(memory_space=pltpu.HBM)],
        out_specs=tuple(whole(2)),
        scratch_shapes=[pltpu.SemaphoreType.DMA((2 * count,))],
        compiler_params=params(),
        name="first_gram",
    )(numbers(pair, xi), pltpu.with_memory_space_constraint(slab, pltpu.HBM))


def second_gram_kernel(idx_ref, slab_ref, out_ref):
    columns = pl.ds(pl.multiple_of(idx_ref[0] * PAIR, PAIR), PAIR)
    total = None
    for tile in row_tiles(slab_ref.shape[0]):
        new = products(slab_ref[tile, columns])
        total = new if total is None else [x + y for x, y in zip(total, new)]
    pack(total, idx_ref[1], out_ref)


def second_gram(slab, pair, xi):
    return pl.pallas_call(
        second_gram_kernel,
        out_shape=pltpu.VMEM((XS * SPAN, T), F32),
        in_specs=[SCALARS] + whole(1),
        out_specs=whole(1)[0],
        compiler_params=params(),
        name="second_gram",
    )(numbers(pair, xi), slab)


def inverse(gramian, eye):
    top = jnp.sqrt(jnp.sum(gramian * gramian))
    scale = 2.0 / (2.0 + top)
    rest = eye - scale * (eye + gramian)

    def rates(gap):
        rate = 1.0 - gap
        grown = 2.0 * gap * (2.0 - gap) / (1.0 + gap * (2.0 - gap))
        return 2.0 / (2.0 - rate * rate), grown

    def more(state):
        count, gap, _, _ = state
        return (gap < 1.0 - ENOUGH) & (count < 60)

    def step(state):
        count, gap, rest, approx = state
        c, gap = rates(gap)
        parts = split(rest)
        square = mul(parts, parts)
        approx = c * (approx + mul(split(approx), parts))
        return count + 1, gap, c * square + (1.0 - c) * eye, approx

    c, gap = rates(scale)
    parts = split(rest)
    approx = (c * scale) * (eye + rest)
    rest = c * mul(parts, parts) + (1.0 - c) * eye
    _, gap, rest, approx = lax.while_loop(more, step, (jnp.int32(0), gap, rest, approx))
    c, _ = rates(gap)
    return c * (approx + mul(split(approx), split(rest)))


def turn(parts):
    return parts[0].T, parts[1].T


def side_by_side(blocks):
    return jnp.concatenate([jnp.concatenate(row, axis=1) for row in blocks], axis=0)


def stacked(blocks):
    return tuple(side_by_side([[b[i] for b in row] for row in blocks]) for i in range(2))


def negative(parts):
    return -parts[0], -parts[1]


def rotation_kernel(
    idx_ref, g0_ref, g1_ref, g2_ref, g3_ref, out_ref, pack_ref, h_ref, e_ref
):
    xi = idx_ref[0]
    for i, ref in enumerate((g0_ref, g1_ref, g2_ref, g3_ref)):
        place = lax.rem(xi - i + XS, XS) * CHUNK
        pack_ref[pl.ds(pl.multiple_of(place, PIECE), CHUNK), :] = ref[:CHUNK, :]
    for b, (row, col) in enumerate(BLOCKS):
        block = pack_ref[b * T : (b + 1) * T, :]
        h_ref[row * T : (row + 1) * T, col * T : (col + 1) * T] = block
        if row != col:
            h_ref[col * T : (col + 1) * T, row * T : (row + 1) * T] = block.T
    rows = lax.broadcasted_iota(jnp.int32, (B, B), 0)
    cols = lax.broadcasted_iota(jnp.int32, (B, B), 1)
    eye = jnp.where(rows == cols, 1.0, 0.0).astype(F32)
    hpp, hpq, hqq = h_ref[:B, :B], h_ref[:B, B:], h_ref[B:, B:]

    for sweep in range(INNER):
        trace = jnp.sum((hpp + hqq) * eye)
        mean = trace / PAIR + 1e-6
        factor = -1.0 / (mean * mean)
        pq = split(hpq)
        x = split((mul(split(hpp), pq) - mul(pq, split(hqq))) * factor)
        xt = turn(x)
        pi = inverse(mul(x, xt), eye)
        w = mul(split(pi), x)
        ws = split(2.0 * w)
        wt = turn(ws)
        corner = split(2.0 * (pi - eye))
        t = split(mul(xt, negative(ws)))
        e = stacked([[corner, ws], [negative(wt), t]])
        if sweep + 1 < INNER:
            h = h_ref[...]
            m = h + mul(split(h), e)
            left, right = split(m[:, :B]), split(m[:, B:])
            low = stacked([[corner, negative(ws)]])
            high = stacked([[wt, t]])
            hpp = m[:B, :B] + mul(low, left)
            hpq = m[:B, B:] + mul(low, right)
            hqq = m[B:, B:] + mul(high, right)
            for i in range(2):
                e_ref[i] = e[i]
        else:
            first = e_ref[0], e_ref[1]
            plain = first[0].astype(F32) + first[1].astype(F32)
            both = e[0].astype(F32) + e[1].astype(F32)
            r = lax.broadcasted_iota(jnp.int32, (PAIR, PAIR), 0)
            c = lax.broadcasted_iota(jnp.int32, (PAIR, PAIR), 1)
            unit = jnp.where(r == c, 1.0, 0.0).astype(F32)
            out_ref[...] = (unit + (plain + both) + mul(first, e)).astype(BF)


def rotation(chunks, xi):
    spec = pl.BlockSpec((SPAN, T), lambda i, idx: (0, 0))
    return pl.pallas_call(
        rotation_kernel,
        out_shape=jax.ShapeDtypeStruct((PAIR, PAIR), BF),
        grid_spec=pltpu.PrefetchScalarGridSpec(
            num_scalar_prefetch=1,
            grid=(1,),
            in_specs=[spec] * XS,
            out_specs=pl.BlockSpec((PAIR, PAIR), lambda i, idx: (0, 0)),
            scratch_shapes=[
                pltpu.VMEM((PACKED, T), F32),
                pltpu.VMEM((PAIR, PAIR), F32),
                pltpu.VMEM((2, PAIR, PAIR), BF),
            ],
        ),
        compiler_params=params(24),
        name="rotation",
    )(xi.reshape(1).astype(jnp.int32), *chunks)


def edge_kernel(idx_ref, a_ref, rot_ref, out_ref):
    columns = pl.ds(pl.multiple_of(idx_ref[0] * PAIR, PAIR), PAIR)
    rot = rot_ref[:, pl.ds(pl.multiple_of(idx_ref[1] * B, B), B)]
    for tile in row_tiles(a_ref.shape[0]):
        out_ref[tile, :] = dot(a_ref[tile, columns], rot).astype(BF)


def edge(slab, rot, pair, half):
    return pl.pallas_call(
        edge_kernel,
        out_shape=pltpu.VMEM((slab.shape[0], B), BF),
        in_specs=[SCALARS] + whole(2),
        out_specs=whole(1)[0],
        compiler_params=params(),
        name="edge",
    )(numbers(pair, half), slab, rot)


def inner_kernel(last, idx_ref, a_ref, own_ref, other_ref, first_ref, out_ref, rot_ref, stage_ref, sems):
    core, position = idx_ref[0], idx_ref[1]
    tiles = row_tiles(a_ref.shape[0])

    def arrived(side):
        return pltpu.make_async_copy(
            first_ref, out_ref.at[:, pl.ds(side * (PAIR + B), B)], sems.at[len(tiles)]
        )

    def ended(i, side):
        columns = pl.ds(side * (PAIR + B), B)
        return pltpu.make_async_copy(
            stage_ref.at[tiles[i], columns],
            out_ref.at[tiles[i], columns],
            sems.at[len(tiles) + 1 + i],
        )

    goes = ((core == 1) & (position > 0), (core == 0) & (position < last))
    for side in range(2):

        @pl.when(goes[side])
        def _():
            arrived(side).start()

    rot_ref[core] = own_ref[...]
    rot_ref[1 - core] = other_ref[...]
    kept = rot_ref[1, :, B:]
    passed = rot_ref[0, :, pl.ds(pl.multiple_of(jnp.where(position == 0, B, 0), B), B)]
    middle = pl.ds(B, PAIR)
    copies = []
    for i, tile in enumerate(tiles):
        stage_ref[tile, B:PAIR] = dot(a_ref[tile, PAIR:], kept).astype(BF)
        stage_ref[tile, PAIR : PAIR + B] = dot(a_ref[tile, :PAIR], passed).astype(BF)
        copies.append(
            pltpu.make_async_copy(
                stage_ref.at[tile, middle], out_ref.at[tile, middle], sems.at[i]
            )
        )
        copies[-1].start()
    for side, place in ((0, 0), (1, last)):

        @pl.when(position == place)
        def _():
            rot = rot_ref[side, :, :B]
            for i, tile in enumerate(tiles):
                pair = a_ref[tile, side * PAIR : (side + 1) * PAIR]
                columns = slice(side * (PAIR + B), side * (PAIR + B) + B)
                stage_ref[tile, columns] = dot(pair, rot).astype(BF)
                ended(i, side).start()
            for i in range(len(tiles)):
                ended(i, side).wait()

    for copy in copies:
        copy.wait()
    for side in range(2):

        @pl.when(goes[side])
        def _():
            arrived(side).wait()


def inner(slab, own, other, first, core, position, last):
    count = slab.shape[0] // ROW_TILE
    return pl.pallas_call(
        lambda *refs: inner_kernel(last, *refs),
        out_shape=jax.ShapeDtypeStruct(slab.shape, BF),
        in_specs=[SCALARS] + whole(4),
        out_specs=ANYWHERE,
        scratch_shapes=[
            pltpu.VMEM((2, PAIR, PAIR), BF),
            pltpu.VMEM(slab.shape, BF),
            pltpu.SemaphoreType.DMA((2 * count + 1,)),
        ],
        compiler_params=params(),
        name="inner",
    )(numbers(core, position), slab, own, other, first)


def place_kernel(last, idx_ref, block_ref, part_ref, out_ref, sem):
    del part_ref
    core, position = idx_ref[0], idx_ref[1]
    goes = ((core == 0) & (position > 0), (core == 1) & (position < last))
    for side in range(2):

        @pl.when(goes[side])
        def _():
            copy = pltpu.make_async_copy(
                block_ref, out_ref.at[:, pl.ds(side * (PAIR + B), B)], sem.at[0]
            )
            copy.start()
            copy.wait()


def place(part, block, core, position, last):
    return pl.pallas_call(
        lambda *refs: place_kernel(last, *refs),
        out_shape=jax.ShapeDtypeStruct(part.shape, part.dtype),
        in_specs=[SCALARS] + whole(1) + [ANYWHERE],
        out_specs=ANYWHERE,
        scratch_shapes=[pltpu.SemaphoreType.DMA((1,))],
        input_output_aliases={2: 0},
        compiler_params=params(),
        name="place",
    )(numbers(core, position), block, part)


def shifted(array, axis, by):
    size = lax.axis_size(axis)
    return lax.ppermute(array, axis, [(i, (i + by) % size) for i in range(size)])


def along_chain(array, ups):
    size = lax.axis_size(("blk", "grp"))
    moves = []
    for core in range(2):
        for i in range(size - 1):
            pair = (core * size + i, core * size + i + 1)
            moves.append(pair if core in ups else pair[::-1])
    return lax.ppermute(array, ("core", "blk", "grp"), moves)


def encode(chunk):
    exponent = jnp.floor(jnp.log2(jnp.maximum(chunk[CHUNK : CHUNK + 1], 1e-30))) + 1.0
    rows = lax.broadcasted_iota(jnp.int32, chunk.shape, 0)
    scaled = chunk * jnp.exp2(TOP_EXPONENT - exponent)
    return jnp.where(rows < CHUNK, scaled, exponent).astype(jnp.float16)


def decode(message):
    message = message.astype(F32)
    exponent = message[CHUNK : CHUNK + 1]
    rows = lax.broadcasted_iota(jnp.int32, message.shape, 0)
    value = message * jnp.exp2(exponent - TOP_EXPONENT)
    return jnp.where(rows < CHUNK, value, jnp.exp2(exponent))


def body(slab):
    core, xi = lax.axis_index("core"), lax.axis_index("x")
    chain = ("blk", "grp")
    last, position = lax.axis_size(chain) - 1, lax.axis_index(chain)

    theirs, slab = first_gram(slab, 1 - core, xi)
    received = shifted(theirs, "core", 1)
    packed = second_gram(slab, core, xi) + received

    total, *rest = (packed[i * SPAN : (i + 1) * SPAN] for i in range(XS))
    parts = [shifted(encode(part), "x", i) for i, part in enumerate(rest, 1)]
    for part in parts:
        total = total + decode(part)
    total = total + decode(shifted(encode(total), "yh", 1))
    coded = encode(total)
    chunks = [total] + [decode(shifted(coded, "x", i)) for i in range(1, XS)]

    own = rotation(chunks, xi)
    first = edge(slab, own, core, 1 - core)
    first = along_chain(first, (1,))
    other = shifted(own, "core", 1)
    second = edge(slab, other, 1 - core, core)
    second = along_chain(second, (0,))
    out = inner(slab, own, other, first, core, position, last)
    return place(out, second, core, position, last)


def solution(mesh):
    rows, blk, grp = (mesh.shape[name] for name in ("row", "blk", "grp"))
    fine = Mesh(
        mesh.devices.reshape(rows // (2 * XS), XS, 2, blk, grp),
        ("yh", "x", "core", "blk", "grp"),
    )
    spec = P(("yh", "x", "core"), ("blk", "grp"))
    return jax.shard_map(
        body, mesh=fine, in_specs=(spec,), out_specs=spec, check_vma=False
    )
```

```python
import jax
import jax.numpy as jnp
from jax import lax
from jax.experimental import pallas as pl
from jax.experimental.pallas import tpu as pltpu
from jax.sharding import Mesh, PartitionSpec as P


B = 256
PAIR = 2 * B
INNER = 2
T = 128
BLOCKS = ((0, 0), (0, 1), (1, 1), (0, 2), (0, 3), (1, 2), (1, 3), (2, 2), (2, 3), (3, 3))
PACKED = len(BLOCKS) * T
XS = 4
CHUNK = PACKED // XS
PIECE = 64
TAIL = 16
SPAN = CHUNK + TAIL
BF = jnp.bfloat16
F32 = jnp.float32
ROW_TILE = 512
TOP_EXPONENT = 14.0
ENOUGH = 1e-2


def params(mib=8):
    return pltpu.CompilerParams(vmem_limit_bytes=mib << 20)


def dot(a, b):
    return lax.dot_general(a, b, (((1,), (0,)), ((), ())), preferred_element_type=F32)


def dot_tn(a, b):
    return lax.dot_general(a, b, (((0,), (0,)), ((), ())), preferred_element_type=F32)


def split(x):
    hi = x.astype(BF)
    return hi, (x - hi.astype(F32)).astype(BF)


def mul(a, b):
    left = jnp.concatenate([a[0], a[0], a[1]], axis=1)
    return dot(left, jnp.concatenate([b[0], b[1], b[0]], axis=0))


def whole(count):
    return [pl.BlockSpec(memory_space=pltpu.VMEM)] * count


def numbers(*values):
    return jnp.stack(values).astype(jnp.int32)


SCALARS = pl.BlockSpec(memory_space=pltpu.SMEM)
ANYWHERE = pl.BlockSpec(memory_space=pl.ANY)


def row_tiles(rows):
    return [pl.ds(i * ROW_TILE, ROW_TILE) for i in range(rows // ROW_TILE)]


def pack(acc, xi, out_ref):
    top = jnp.zeros((TAIL, T), F32)
    for q in range(PACKED // PIECE):
        row, col = BLOCKS[q * PIECE // T]
        part = q * PIECE % T
        which = row // 2 + col // 2
        r0, c0 = row % 2 * T + part, col % 2 * T
        chunk, offset = divmod(q * PIECE, CHUNK)
        place = lax.rem(chunk - xi + XS, XS) * SPAN + offset
        piece = acc[which][r0 : r0 + PIECE, c0 : c0 + T]
        out_ref[pl.ds(pl.multiple_of(place, TAIL), PIECE), :] = piece
        for r in range(0, PIECE, TAIL):
            top = jnp.maximum(top, jnp.abs(piece[r : r + TAIL]))
    top = jnp.broadcast_to(jnp.max(top, axis=0, keepdims=True), (TAIL, T))
    for i in range(XS):
        out_ref[i * SPAN + CHUNK : (i + 1) * SPAN, :] = top


def products(rows):
    upper, lower = rows[:, :B], rows[:, B:]
    return dot_tn(upper, upper), dot_tn(upper, lower), dot_tn(lower, lower)


def first_gram_kernel(idx_ref, a_ref, out_ref, first_ref, second_ref, sems):
    pair, xi = idx_ref[0], idx_ref[1]
    tiles = row_tiles(a_ref.shape[0])

    def fetch(i, second):
        which = 1 - pair if second else pair
        columns = pl.ds(pl.multiple_of(which * PAIR, PAIR), PAIR)
        target = second_ref if second else first_ref
        return pltpu.make_async_copy(
            a_ref.at[tiles[i], columns],
            target.at[tiles[i], :],
            sems.at[i + second * len(tiles)],
        )

    for second in range(2):
        for i in range(len(tiles)):
            fetch(i, second).start()
    total = None
    for i, tile in enumerate(tiles):
        fetch(i, 0).wait()
        new = products(first_ref[tile, :])
        total = new if total is None else [x + y for x, y in zip(total, new)]
    pack(total, xi, out_ref)
    for i in range(len(tiles)):
        fetch(i, 1).wait()


def first_gram(slab, pair, xi):
    count = slab.shape[0] // ROW_TILE
    half = (slab.shape[0], PAIR)
    return pl.pallas_call(
        first_gram_kernel,
        out_shape=(
            pltpu.VMEM((XS * SPAN, T), F32),
            pltpu.VMEM(half, slab.dtype),
            pltpu.VMEM(half, slab.dtype),
        ),
        in_specs=[SCALARS, pl.BlockSpec(memory_space=pltpu.HBM)],
        out_specs=tuple(whole(3)),
        scratch_shapes=[pltpu.SemaphoreType.DMA((2 * count,))],
        compiler_params=params(),
        name="first_gram",
    )(numbers(pair, xi), pltpu.with_memory_space_constraint(slab, pltpu.HBM))


def second_gram_kernel(idx_ref, slab_ref, out_ref):
    total = None
    for tile in row_tiles(slab_ref.shape[0]):
        new = products(slab_ref[tile, :])
        total = new if total is None else [x + y for x, y in zip(total, new)]
    pack(total, idx_ref[0], out_ref)


def second_gram(slab, xi):
    return pl.pallas_call(
        second_gram_kernel,
        out_shape=pltpu.VMEM((XS * SPAN, T), F32),
        in_specs=[SCALARS] + whole(1),
        out_specs=whole(1)[0],
        compiler_params=params(),
        name="second_gram",
    )(numbers(xi), slab)


def inverse(gramian, eye):
    top = jnp.sqrt(jnp.sum(gramian * gramian))
    scale = 2.0 / (2.0 + top)
    rest = eye - scale * (eye + gramian)

    def rates(gap):
        rate = 1.0 - gap
        grown = 2.0 * gap * (2.0 - gap) / (1.0 + gap * (2.0 - gap))
        return 2.0 / (2.0 - rate * rate), grown

    def more(state):
        count, gap, _, _ = state
        return (gap < 1.0 - ENOUGH) & (count < 60)

    def step(state):
        count, gap, rest, approx = state
        c, gap = rates(gap)
        parts = split(rest)
        square = mul(parts, parts)
        approx = c * (approx + mul(split(approx), parts))
        return count + 1, gap, c * square + (1.0 - c) * eye, approx

    c, gap = rates(scale)
    parts = split(rest)
    approx = (c * scale) * (eye + rest)
    rest = c * mul(parts, parts) + (1.0 - c) * eye
    _, gap, rest, approx = lax.while_loop(more, step, (jnp.int32(0), gap, rest, approx))
    c, _ = rates(gap)
    return c * (approx + mul(split(approx), split(rest)))


def turn(parts):
    return parts[0].T, parts[1].T


def side_by_side(blocks):
    return jnp.concatenate([jnp.concatenate(row, axis=1) for row in blocks], axis=0)


def stacked(blocks):
    return tuple(side_by_side([[b[i] for b in row] for row in blocks]) for i in range(2))


def negative(parts):
    return -parts[0], -parts[1]


def rotation_kernel(
    idx_ref, g0_ref, g1_ref, g2_ref, g3_ref, out_ref, edge_ref, pack_ref, h_ref, e_ref
):
    xi, core = idx_ref[0], idx_ref[1]
    for i, ref in enumerate((g0_ref, g1_ref, g2_ref, g3_ref)):
        place = lax.rem(xi - i + XS, XS) * CHUNK
        pack_ref[pl.ds(pl.multiple_of(place, PIECE), CHUNK), :] = ref[:CHUNK, :]
    for b, (row, col) in enumerate(BLOCKS):
        block = pack_ref[b * T : (b + 1) * T, :]
        h_ref[row * T : (row + 1) * T, col * T : (col + 1) * T] = block
        if row != col:
            h_ref[col * T : (col + 1) * T, row * T : (row + 1) * T] = block.T
    rows = lax.broadcasted_iota(jnp.int32, (B, B), 0)
    cols = lax.broadcasted_iota(jnp.int32, (B, B), 1)
    eye = jnp.where(rows == cols, 1.0, 0.0).astype(F32)
    hpp, hpq, hqq = h_ref[:B, :B], h_ref[:B, B:], h_ref[B:, B:]

    for sweep in range(INNER):
        trace = jnp.sum((hpp + hqq) * eye)
        mean = trace / PAIR + 1e-6
        factor = -1.0 / (mean * mean)
        pq = split(hpq)
        x = split((mul(split(hpp), pq) - mul(pq, split(hqq))) * factor)
        xt = turn(x)
        pi = inverse(mul(x, xt), eye)
        w = mul(split(pi), x)
        ws = split(2.0 * w)
        wt = turn(ws)
        corner = split(2.0 * (pi - eye))
        t = split(mul(xt, negative(ws)))
        e = stacked([[corner, ws], [negative(wt), t]])
        if sweep + 1 < INNER:
            h = h_ref[...]
            m = h + mul(split(h), e)
            left, right = split(m[:, :B]), split(m[:, B:])
            low = stacked([[corner, negative(ws)]])
            high = stacked([[wt, t]])
            hpp = m[:B, :B] + mul(low, left)
            hpq = m[:B, B:] + mul(low, right)
            hqq = m[B:, B:] + mul(high, right)
            for i in range(2):
                e_ref[i] = e[i]
        else:
            first = e_ref[0], e_ref[1]
            plain = first[0].astype(F32) + first[1].astype(F32)
            both = e[0].astype(F32) + e[1].astype(F32)
            r = lax.broadcasted_iota(jnp.int32, (PAIR, PAIR), 0)
            c = lax.broadcasted_iota(jnp.int32, (PAIR, PAIR), 1)
            unit = jnp.where(r == c, 1.0, 0.0).astype(F32)
            out_ref[...] = (unit + (plain + both) + mul(first, e)).astype(BF)
            half = pl.ds(pl.multiple_of((1 - core) * B, B), B)
            edge_ref[...] = out_ref[:, half]


def rotation(chunks, xi, core):
    spec = pl.BlockSpec((SPAN, T), lambda i, idx: (0, 0))
    return pl.pallas_call(
        rotation_kernel,
        out_shape=(
            jax.ShapeDtypeStruct((PAIR, PAIR), BF),
            jax.ShapeDtypeStruct((PAIR, B), BF),
        ),
        grid_spec=pltpu.PrefetchScalarGridSpec(
            num_scalar_prefetch=1,
            grid=(1,),
            in_specs=[spec] * XS,
            out_specs=(
                pl.BlockSpec((PAIR, PAIR), lambda i, idx: (0, 0)),
                pl.BlockSpec((PAIR, B), lambda i, idx: (0, 0)),
            ),
            scratch_shapes=[
                pltpu.VMEM((PACKED, T), F32),
                pltpu.VMEM((PAIR, PAIR), F32),
                pltpu.VMEM((2, PAIR, PAIR), BF),
            ],
        ),
        compiler_params=params(24),
        name="rotation",
    )(numbers(xi, core), *chunks)


def inner_kernel(last, idx_ref, mine_ref, theirs_ref, own_ref, other_ref, out_ref, stage_ref, sems):
    core, position = idx_ref[0], idx_ref[1]
    tiles = row_tiles(mine_ref.shape[0])
    pairs = ((mine_ref, theirs_ref), (theirs_ref, mine_ref))
    rots = ((own_ref, other_ref), (other_ref, own_ref))
    half = pl.ds(pl.multiple_of(jnp.where(position == 0, B, 0), B), B)

    def move(i, start, width):
        columns = pl.ds(start, width)
        return pltpu.make_async_copy(
            stage_ref.at[tiles[i], columns],
            out_ref.at[tiles[i], columns],
            sems.at[i + (width == B) * len(tiles)],
        )

    for c in range(2):

        @pl.when(core == c)
        def _():
            kept = rots[c][1][:, B:]
            passed = rots[c][0][:, half]
            for i, tile in enumerate(tiles):
                stage_ref[tile, B:PAIR] = dot(pairs[c][1][tile, :], kept).astype(BF)
                stage_ref[tile, PAIR : PAIR + B] = dot(pairs[c][0][tile, :], passed).astype(BF)
                move(i, B, PAIR).start()

        for side, place in ((0, 0), (1, last)):

            @pl.when((core == c) & (position == place))
            def _():
                start = side * (PAIR + B)
                rot = rots[c][side][:, :B]
                for i, tile in enumerate(tiles):
                    block = dot(pairs[c][side][tile, :], rot)
                    stage_ref[tile, start : start + B] = block.astype(BF)
                    move(i, start, B).start()
                for i in range(len(tiles)):
                    move(i, start, B).wait()

    for i in range(len(tiles)):
        move(i, B, PAIR).wait()


def inner(mine, theirs, own, other, core, position, last):
    rows = mine.shape[0]
    shape = (rows, 2 * PAIR)
    return pl.pallas_call(
        lambda *refs: inner_kernel(last, *refs),
        out_shape=jax.ShapeDtypeStruct(shape, BF),
        in_specs=[SCALARS] + whole(4),
        out_specs=ANYWHERE,
        scratch_shapes=[
            pltpu.VMEM(shape, BF),
            pltpu.SemaphoreType.DMA((2 * rows // ROW_TILE,)),
        ],
        compiler_params=params(),
        name="inner",
    )(numbers(core, position), mine, theirs, own, other)


def outer_kernel(last, seam, idx_ref, near_ref, far_ref, rot_ref, part_ref, out_ref, stage_ref, sems):
    del part_ref
    high, position = idx_ref[0], idx_ref[1]
    tiles = row_tiles(near_ref.shape[0])

    def move(i, side):
        return pltpu.make_async_copy(
            stage_ref.at[tiles[i], :],
            out_ref.at[tiles[i], pl.ds(side * (PAIR + B), B)],
            sems.at[i],
        )

    for side in range(2):
        chosen = (high == side) & (position != (last if side else 0))
        met = position == (seam - 1 if side else seam)
        for ref, when in ((near_ref, jnp.logical_not(met)), (far_ref, met)):

            @pl.when(chosen & when)
            def _():
                for i, tile in enumerate(tiles):
                    stage_ref[tile, :] = dot(ref[tile, :], rot_ref[...]).astype(BF)
                    move(i, side).start()
                for i in range(len(tiles)):
                    move(i, side).wait()


def outer(part, near, far, rot, high, position, last, seam):
    rows = near.shape[0]
    return pl.pallas_call(
        lambda *refs: outer_kernel(last, seam, *refs),
        out_shape=jax.ShapeDtypeStruct(part.shape, part.dtype),
        in_specs=[SCALARS] + whole(3) + [ANYWHERE],
        out_specs=ANYWHERE,
        scratch_shapes=[
            pltpu.VMEM((rows, B), BF),
            pltpu.SemaphoreType.DMA((rows // ROW_TILE,)),
        ],
        input_output_aliases={4: 0},
        compiler_params=params(),
        name="outer",
    )(numbers(high, position), near, far, rot, part)


def shifted(array, axis, by):
    size = lax.axis_size(axis)
    return lax.ppermute(array, axis, [(i, (i + by) % size) for i in range(size)])


def along_chain(array, ups, steps):
    size = lax.axis_size(("blk", "grp"))
    moves = []
    for core in range(2):
        for i in steps:
            pair = (core * size + i, core * size + i + 1)
            moves.append(pair if core in ups else pair[::-1])
    return lax.ppermute(array, ("core", "blk", "grp"), moves)


def across(array, steps):
    size = lax.axis_size(("blk", "grp"))
    moves = []
    for core in range(2):
        for i in steps:
            pair = (core * size + i, core * size + i + 1)
            moves += [pair, pair[::-1]]
    return lax.ppermute(array, ("core", "blk", "grp"), moves)


def encode(chunk):
    exponent = jnp.floor(jnp.log2(jnp.maximum(chunk[CHUNK : CHUNK + 1], 1e-30))) + 1.0
    rows = lax.broadcasted_iota(jnp.int32, chunk.shape, 0)
    scaled = chunk * jnp.exp2(TOP_EXPONENT - exponent)
    return jnp.where(rows < CHUNK, scaled, exponent).astype(jnp.float16)


def decode(message):
    message = message.astype(F32)
    exponent = message[CHUNK : CHUNK + 1]
    rows = lax.broadcasted_iota(jnp.int32, message.shape, 0)
    value = message * jnp.exp2(exponent - TOP_EXPONENT)
    return jnp.where(rows < CHUNK, value, jnp.exp2(exponent))


def body(slab):
    core, xi = lax.axis_index("core"), lax.axis_index("x")
    chain = ("blk", "grp")
    size, position = lax.axis_size(chain), lax.axis_index(chain)
    last, seam = size - 1, lax.axis_size("grp")
    near = [i for i in range(last) if (i + 1) % seam]
    far = [i for i in range(last) if (i + 1) % seam == 0]

    theirs, their_slab, my_slab = first_gram(slab, 1 - core, xi)
    received = shifted(theirs, "core", 1)
    packed = second_gram(my_slab, xi) + received

    total, *rest = (packed[i * SPAN : (i + 1) * SPAN] for i in range(XS))
    parts = []
    for i, part in enumerate(rest, 1):
        parts.append(shifted(encode(part), "x", i))
    their_near = along_chain(their_slab, (0,), near)
    for part in parts:
        total = total + decode(part)
    total = total + decode(shifted(encode(total), "yh", 1))
    my_near = along_chain(my_slab, (1,), near)
    coded = encode(total)
    takes = (position % seam == seam - 1) == (core == 0)
    chosen = jnp.where(takes, their_slab, my_slab)
    chunks = [total]
    for i in range(1, XS):
        chunks.append(decode(shifted(coded, "x", i)))
    far_slab = across(chosen, far)

    own, edge = rotation(chunks, xi, core)
    other = shifted(own, "core", 1)
    from_side = along_chain(edge, (1,), range(last))
    out = inner(my_slab, their_slab, own, other, core, position, last)
    from_core = shifted(from_side, "core", 1)
    out = outer(out, my_near, far_slab, from_side, 1 - core, position, last, seam)
    return outer(out, their_near, far_slab, from_core, core, position, last, seam)


def solution(mesh):
    rows, blk, grp = (mesh.shape[name] for name in ("row", "blk", "grp"))
    fine = Mesh(
        mesh.devices.reshape(rows // (2 * XS), XS, 2, blk, grp),
        ("yh", "x", "core", "blk", "grp"),
    )
    spec = P(("yh", "x", "core"), ("blk", "grp"))
    return jax.shard_map(
        body, mesh=fine, in_specs=(spec,), out_specs=spec, check_vma=False
    )
```
